32 devices in a mesh: grid: 8 (over y, x, core), ipts: 4 (over z).
Axes of the slice: x: 2, y: 2, z: 4, core: 2. Of those that a mesh axis runs over, the one named last changes fastest.
Arguments:
- orbitals: bfloat16 [16384, 1024], P(('grid', 'ipts')), may hold values from -1.1953125 to 1.1953125
- targets: bfloat16 [16384, 256], P(('grid', 'ipts')), may hold values from -6 to 6
- points: int32 [4, 1024], P('ipts', 'grid'), may hold values from 0 to 16383, as said below
- potential: bfloat16 [16384, 4096], P('grid', 'ipts'), may hold values from -0.09375 to 0.09375
Outputs:
- exchanged: bfloat16 [16384, 256], P(('grid', 'ipts'))
The draws below stay inside these ranges and needn't reach their ends.
Inputs may be any that keep to these rules, and one draw needn't show every extreme that they name: Indices are distinct over all groups; each row of points rises strictly, and its entries k * 128 to (k + 1) * 128 - 1 lie in grid rows k * 2048 to (k + 1) * 2048 - 1.
All inputs are finite; a program needn't handle non-finite values.
Results may differ from the reference program's by a relative error of at most 0.0049.
Values may be sent and summed in bfloat16 or wider, within the bound.
A program may use at most 128 MiB of HBM per device.

```python
import jax
import jax.numpy as jnp
from jax import lax

NORB = 1024
NJ = 256
PTS_SLAB = 128
SLAB = 2048
GROUPS = 4
PER_GROUP = 1024
NG = 16384
NMU = 4096


def draw_points(key, part):
    slabs = PER_GROUP // PTS_SLAB
    keys = jax.random.split(jax.random.fold_in(key, 7), slabs)

    def one_slab(slab_key):
        order = jax.random.permutation(slab_key, SLAB)
        chosen = order[:GROUPS * PTS_SLAB].reshape(GROUPS, PTS_SLAB)
        return jnp.sort(chosen, axis=1).astype(jnp.int32)
    picks = jax.vmap(one_slab)(keys)
    offsets = (jnp.arange(slabs, dtype=jnp.int32) * SLAB)[:, None, None]
    return jnp.transpose(picks + offsets, (1, 0, 2)).reshape(GROUPS, PER_GROUP)


def steps_of(own_key, extent, cuts, low, top_value):
    gain = 1.0
    for position, parts in cuts:
        draws = jax.random.uniform(jax.random.fold_in(jax.random.fold_in(own_key, 6), position), (parts,), jnp.float32, low / len(cuts), top_value / len(cuts))
        gain = gain * jnp.repeat(jnp.exp(draws), extent[position] // parts).reshape((-1,) + (1,) * (len(extent) - 1 - position))
    return gain


def scatter_about(key, extent, deviation, bound, cuts=(), kind=jnp.bfloat16):
    factor_of = steps_of(key, extent, cuts, -0.22, 0.18) if cuts else 1.0
    values = jax.random.normal(key, extent, jnp.float32) * deviation * factor_of
    return jnp.minimum(jnp.maximum(values, -bound), bound).astype(kind)


def setup_inputs(seed: int = 0) -> dict:
    splits = jax.random.split(jax.random.key(seed), 5)
    orbitals = scatter_about(splits[0], (NG, NORB), 0.2, 1.1953125, ((0, 32),))
    targets = scatter_about(splits[1], (NG, NJ), 1.0, 6.0, ((0, 32),))
    points = draw_points(jax.random.fold_in(splits[4], 71), 0)
    potential = scatter_about(splits[3], (NG, NMU), (4 * PER_GROUP) ** -0.5, 0.09375, ((0, 8), (1, 4)))
    return dict(orbitals=orbitals, targets=targets, points=points, potential=potential)


def reference(orbitals, targets, points, potential):
    slabs = NG // SLAB
    values = []
    for group in range(GROUPS):
        index = points[group]
        values.append((jnp.take(orbitals, index, axis=0), jnp.take(targets, index, axis=0)))

    def one_slab(slab_index):
        start = slab_index * SLAB
        rows = lax.dynamic_slice_in_dim(orbitals, start, SLAB, 0)
        kernel_rows = lax.dynamic_slice_in_dim(potential, start, SLAB, 0)
        total = jnp.zeros((SLAB, NJ), jnp.float32)
        for group in range(GROUPS):
            orbital_values, target_values = values[group]
            products = lax.dot_general(rows, orbital_values, (((1,), (1,)), ((), ())), preferred_element_type=jnp.float32)
            kernel = kernel_rows[:, group * PER_GROUP:(group + 1) * PER_GROUP].astype(jnp.float32)
            weighted = (kernel * products).astype(jnp.bfloat16)
            total = total + jnp.dot(weighted, target_values, preferred_element_type=jnp.float32)
        return (-total).astype(jnp.bfloat16)

    result = lax.map(one_slab, jnp.arange(slabs, dtype=jnp.int32))
    return result.reshape(NG, NJ)
```

```python
import functools

import jax
import jax.numpy as jnp
from jax import lax
from jax.experimental import pallas as pl
from jax.experimental.pallas import tpu as pltpu
from jax.sharding import PartitionSpec as P

MESH = pl.DeviceIdType.MESH
WIDTH = 256


def kernel(groups, slabs, pieces, orbitals, targets, points, potential, out,
           slab, orbital_values, target_values, weights, target_rows, every_group, picked, landed,
           total, leaving, arriving,
           local_sem, up_sem, down_sem, row_sem, grid_send, grid_recv, index_send, index_recv,
           pick_send, pick_recv, value_send, value_recv, sum_send, sum_recv):
    g = lax.axis_index("grid")
    z = lax.axis_index("ipts")
    rows, norb = orbitals.shape
    nj = targets.shape[1]
    count = points.shape[1]
    cut = norb // pieces

    def at(grid, group):
        return {"grid": grid, "ipts": group}

    def other(base, step, size):
        return lax.rem(base + step, size)

    own = [
        pltpu.make_async_copy(
            orbitals.at[:, pl.ds(k * cut, cut)], slab.at[z, :, pl.ds(k * cut, cut)], local_sem.at[k])
        for k in range(pieces)
    ]
    own_targets = pltpu.make_async_copy(targets, target_rows, local_sem.at[pieces])
    own_points = pltpu.make_async_copy(points, every_group.at[0], local_sem.at[pieces + 1])
    own_weights = pltpu.make_async_copy(potential, weights, local_sem.at[pieces + 2])
    own_points.start()
    for copy in own:
        copy.start()
    own_targets.start()
    own_weights.start()

    barrier = pltpu.get_barrier_semaphore()
    for step in range(1, groups):
        pl.semaphore_signal(barrier, inc=1, device_id=at(g, other(z, step, groups)), device_id_type=MESH)
    for step in range(1, slabs):
        pl.semaphore_signal(barrier, inc=1, device_id=at(other(g, step, slabs), z), device_id_type=MESH)
    pl.semaphore_wait(barrier, groups + slabs - 2)

    def line_copy(k, chunk, sem, target):
        block = slab.at[chunk, :, pl.ds(k * cut, cut)]
        return pltpu.make_async_remote_copy(
            src_ref=block, dst_ref=block, send_sem=sem, recv_sem=row_sem.at[k, chunk],
            device_id=at(g, target), device_id_type=MESH)

    def up(k, d):
        return (z - d >= 0) & (z + 1 < groups), line_copy(
            k, jnp.maximum(z - d, 0), up_sem.at[k, d], jnp.minimum(z + 1, groups - 1))

    def down(k, d):
        return (z + d < groups) & (z >= 1), line_copy(
            k, jnp.minimum(z + d, groups - 1), down_sem.at[k, d], jnp.maximum(z - 1, 0))

    def send_line(k, d):
        for valid, copy in (up(k, d), down(k, d)):
            pl.when(valid)(copy.start)

    def await_line(k, d):
        pl.when(z - d >= 0)(lambda: line_copy(k, jnp.maximum(z - d, 0), up_sem.at[k, 0], z).wait_recv())
        pl.when(z + d < groups)(
            lambda: line_copy(k, jnp.minimum(z + d, groups - 1), up_sem.at[k, 0], z).wait_recv())

    own[0].wait()
    send_line(0, 0)
    own_points.wait()
    index_copies = [
        pltpu.make_async_remote_copy(
            src_ref=every_group.at[0], dst_ref=every_group.at[step],
            send_sem=index_send.at[step - 1], recv_sem=index_recv.at[step - 1],
            device_id=at(g, other(z, step, groups)), device_id_type=MESH)
        for step in range(1, groups)
    ]
    for copy in index_copies:
        copy.start()

    slab_start = g * rows * groups

    def chosen(indices, start, length):
        place = lax.broadcasted_iota(jnp.int32, (length, count), 0) + start
        return (place == indices).astype(jnp.float32).astype(jnp.bfloat16)

    def pick(indices, start, block):
        return lax.dot_general(
            chosen(indices, start, block.shape[0]), block, (((0,), (0,)), ((), ())),
            preferred_element_type=jnp.float32)

    own_targets.wait()
    own_start = slab_start + z * rows
    pick_copies = []
    own_pick = pick(every_group[0], own_start, target_rows[...])
    for step in range(1, groups):
        index_copies[step - 1].wait()
        picked[step - 1] = pick(every_group[step], own_start, target_rows[...]).astype(jnp.bfloat16)
        copy = pltpu.make_async_remote_copy(
            src_ref=picked.at[step - 1], dst_ref=landed.at[step - 1],
            send_sem=pick_send.at[step - 1], recv_sem=pick_recv.at[step - 1],
            device_id=at(g, other(z, groups - step, groups)), device_id_type=MESH)
        copy.start()
        pick_copies.append(copy)

    place = pl.ds(pl.multiple_of(g * count, count), count)
    grid_copies = []

    def spread(ref, sends, recvs):
        copies = [
            pltpu.make_async_remote_copy(
                src_ref=ref, dst_ref=ref, send_sem=sends.at[step - 1], recv_sem=recvs.at[step - 1],
                device_id=at(other(g, step, slabs), z), device_id_type=MESH)
            for step in range(1, slabs)
        ]
        for copy in copies:
            copy.start()
        grid_copies.extend(copies)

    for s in range(pieces + groups - 1):
        for d in range(groups):
            k = s - d
            if not 0 <= k < pieces:
                continue
            if d > 0:
                await_line(k, d)
            elif k > 0:
                own[k].wait()
            if d < groups - 1 and s > 0:
                send_line(k, d)
        k = s - (groups - 1)
        if k < 0:
            continue
        columns = pl.ds(k * cut, cut)
        values = jnp.zeros((count, cut), jnp.float32)
        for chunk in range(groups):
            values += pick(every_group[0], slab_start + chunk * rows, slab[chunk, :, columns])
        orbital_values[place, columns] = values.astype(jnp.bfloat16)
        spread(orbital_values.at[place, columns], grid_send.at[k], grid_recv.at[k])
        if k == 0:
            values = own_pick
            for step in range(1, groups):
                pick_copies[step - 1].wait()
                values += landed[step - 1].astype(jnp.float32)
            target_values[place, :] = values.astype(jnp.bfloat16)
            spread(target_values.at[place, :], value_send, value_recv)

    own_weights.wait()
    for copy in grid_copies:
        copy.wait_recv()

    def add_up(chunk):
        total[...] = jnp.zeros_like(total)

        @pl.loop(0, slabs * count // WIDTH)
        def _(b):
            block = pl.ds(pl.multiple_of(b * WIDTH, WIDTH), WIDTH)
            products = lax.dot_general(
                slab[chunk], orbital_values[block, :], (((1,), (1,)), ((), ())),
                preferred_element_type=jnp.float32)
            kernel_rows = weights[pl.ds(pl.multiple_of(chunk * rows, rows), rows), block]
            weighted = (kernel_rows.astype(jnp.float32) * products).astype(jnp.bfloat16)
            total[...] += jnp.dot(weighted, target_values[block, :], preferred_element_type=jnp.float32)

    sum_copies = []
    for n, step in enumerate(range(1, groups)):
        chunk = other(z, step, groups)
        add_up(chunk)
        leaving[n] = total[...].astype(jnp.bfloat16)
        copy = pltpu.make_async_remote_copy(
            src_ref=leaving.at[n], dst_ref=arriving.at[n], send_sem=sum_send.at[n], recv_sem=sum_recv.at[n],
            device_id=at(g, chunk), device_id_type=MESH)
        copy.start()
        sum_copies.append(copy)
    add_up(z)
    summed = total[...]
    for n, copy in enumerate(sum_copies):
        copy.wait_recv()
        summed += arriving[n].astype(jnp.float32)
    out[...] = (-summed).astype(out.dtype)

    for k in range(pieces):
        for d in range(groups - 1):
            for valid, copy in (up(k, d), down(k, d)):
                pl.when(valid)(copy.wait_send)
    for copy in grid_copies + sum_copies:
        copy.wait_send()


def local(orbitals, targets, points, potential):
    groups, slabs = lax.axis_size("ipts"), lax.axis_size("grid")
    rows, norb = orbitals.shape
    nj = targets.shape[1]
    count = points.shape[1]
    pieces = max(norb // 256, 1)
    dma, bf16 = pltpu.SemaphoreType.DMA, jnp.bfloat16
    return pl.pallas_call(
        functools.partial(kernel, groups, slabs, pieces),
        out_shape=jax.ShapeDtypeStruct((rows, nj), bf16),
        in_specs=[pl.BlockSpec(memory_space=pl.ANY)] * 4,
        out_specs=pl.BlockSpec(memory_space=pltpu.VMEM),
        scratch_shapes=[
            pltpu.VMEM((groups, rows, norb), bf16),
            pltpu.VMEM((slabs * count, norb), bf16),
            pltpu.VMEM((slabs * count, nj), bf16),
            pltpu.VMEM(potential.shape, bf16),
            pltpu.VMEM((rows, nj), bf16),
            pltpu.VMEM((groups, 1, count), jnp.int32),
            pltpu.VMEM((groups - 1, count, nj), bf16),
            pltpu.VMEM((groups - 1, count, nj), bf16),
            pltpu.VMEM((rows, nj), jnp.float32),
            pltpu.VMEM((groups - 1, rows, nj), bf16),
            pltpu.VMEM((groups - 1, rows, nj), bf16),
            dma((pieces + 3,)),
            dma((pieces, groups - 1)),
            dma((pieces, groups - 1)),
            dma((pieces, groups)),
            dma((pieces, slabs - 1)),
            dma((pieces, slabs - 1)),
            dma((groups - 1,)),
            dma((groups - 1,)),
            dma((groups - 1,)),
            dma((groups - 1,)),
            dma((slabs - 1,)),
            dma((slabs - 1,)),
            dma((groups - 1,)),
            dma((groups - 1,)),
        ],
        compiler_params=pltpu.CompilerParams(
            collective_id=0, has_side_effects=True, vmem_limit_bytes=60 * 1024 * 1024),
    )(orbitals, targets, points, potential)


def solution(mesh):
    placed = (
        P(("grid", "ipts"), None),
        P(("grid", "ipts"), None),
        P("ipts", "grid"),
        P("grid", "ipts"),
    )
    return jax.shard_map(
        local, mesh=mesh, in_specs=placed, out_specs=P(("grid", "ipts"), None), check_vma=False
    )
```

```python
import functools

import jax
import jax.numpy as jnp
from jax import lax
from jax.experimental import pallas as pl
from jax.experimental.pallas import tpu as pltpu
from jax.sharding import PartitionSpec as P

MESH = pl.DeviceIdType.MESH
WIDTH = 256


def kernel(groups, slabs, pieces, orbitals, targets, points, potential, out,
           slab, orbital_values, target_values, weights, target_rows, every_group, picked, landed,
           total, leaving, arriving, piece_sum, far_leaving, far_values,
           guest_orbitals, guest_targets, guest_weights,
           local_sem, up_sem, down_sem, row_sem, grid_send, grid_recv, index_send, index_recv,
           pick_send, pick_recv, value_send, value_recv, sum_send, sum_recv,
           far_send, far_recv, guest_send, guest_recv, pass_send, pass_recv):
    g = lax.axis_index("grid")
    z = lax.axis_index("ipts")
    rows, norb = orbitals.shape
    nj = targets.shape[1]
    count = points.shape[1]
    cut = norb // pieces
    last = groups - 1
    edge = (z == 0) | (z == last)
    hosting = (z == 1) | (z == last - 1)
    host = jnp.where(z == 0, 1, last - 1)
    far = jnp.where(z == 0, last, 0)
    guest_chunk = jnp.where(z == 1, last, 0)

    def at(grid, group):
        return {"grid": grid, "ipts": group}

    def other(base, step, size):
        return lax.rem(base + step, size)

    own = [
        pltpu.make_async_copy(
            orbitals.at[:, pl.ds(k * cut, cut)], slab.at[z, :, pl.ds(k * cut, cut)], local_sem.at[k])
        for k in range(pieces)
    ]
    own_targets = pltpu.make_async_copy(targets, target_rows, local_sem.at[pieces])
    own_points = pltpu.make_async_copy(points, every_group.at[0], local_sem.at[pieces + 1])
    own_weights = pltpu.make_async_copy(potential, weights, local_sem.at[pieces + 2])
    own_points.start()
    for copy in own:
        copy.start()
    own_targets.start()
    own_weights.start()

    barrier = pltpu.get_barrier_semaphore()
    for step in range(1, groups):
        pl.semaphore_signal(barrier, inc=1, device_id=at(g, other(z, step, groups)), device_id_type=MESH)
    for step in range(1, slabs):
        pl.semaphore_signal(barrier, inc=1, device_id=at(other(g, step, slabs), z), device_id_type=MESH)
    pl.semaphore_wait(barrier, groups + slabs - 2)

    def line_copy(k, chunk, sem, target):
        block = slab.at[chunk, :, pl.ds(k * cut, cut)]
        return pltpu.make_async_remote_copy(
            src_ref=block, dst_ref=block, send_sem=sem, recv_sem=row_sem.at[k, chunk],
            device_id=at(g, target), device_id_type=MESH)

    def up(k, d):
        return (z - d >= 0) & (z + 1 < groups), line_copy(
            k, jnp.maximum(z - d, 0), up_sem.at[k, d], jnp.minimum(z + 1, groups - 1))

    def down(k, d):
        return (z + d < groups) & (z >= 1), line_copy(
            k, jnp.minimum(z + d, groups - 1), down_sem.at[k, d], jnp.maximum(z - 1, 0))

    def send_line(k, d):
        for valid, copy in (up(k, d), down(k, d)):
            pl.when(valid)(copy.start)

    def await_line(k, d):
        pl.when(z - d >= 0)(lambda: line_copy(k, jnp.maximum(z - d, 0), up_sem.at[k, 0], z).wait_recv())
        pl.when(z + d < groups)(
            lambda: line_copy(k, jnp.minimum(z + d, groups - 1), up_sem.at[k, 0], z).wait_recv())

    early = min(2, pieces)
    for copy in own:
        copy.wait()
    send_line(0, 0)

    @pl.when(edge)
    def _():
        for k in range(1, early):
            send_line(k, 0)

    own_points.wait()
    index_copies = [
        pltpu.make_async_remote_copy(
            src_ref=every_group.at[0], dst_ref=every_group.at[step],
            send_sem=index_send.at[step - 1], recv_sem=index_recv.at[step - 1],
            device_id=at(g, other(z, step, groups)), device_id_type=MESH)
        for step in range(1, groups)
    ]
    for copy in index_copies:
        copy.start()

    slab_start = g * rows * groups

    def chosen(indices, start, length):
        place = lax.broadcasted_iota(jnp.int32, (length, count), 0) + start
        return (place == indices).astype(jnp.float32).astype(jnp.bfloat16)

    def pick(indices, start, block):
        return lax.dot_general(
            chosen(indices, start, block.shape[0]), block, (((0,), (0,)), ((), ())),
            preferred_element_type=jnp.float32)

    own_targets.wait()
    own_start = slab_start + z * rows
    pick_copies = []
    own_pick = pick(every_group[0], own_start, target_rows[...])
    for step in range(1, groups):
        index_copies[step - 1].wait()
        picked[step - 1] = pick(every_group[step], own_start, target_rows[...]).astype(jnp.bfloat16)
        copy = pltpu.make_async_remote_copy(
            src_ref=picked.at[step - 1], dst_ref=landed.at[step - 1],
            send_sem=pick_send.at[step - 1], recv_sem=pick_recv.at[step - 1],
            device_id=at(g, other(z, groups - step, groups)), device_id_type=MESH)
        copy.start()
        pick_copies.append(copy)

    far_copies = [
        pltpu.make_async_remote_copy(
            src_ref=far_leaving.at[:, pl.ds(k * cut, cut)], dst_ref=far_values.at[:, pl.ds(k * cut, cut)],
            send_sem=far_send.at[k], recv_sem=far_recv.at[k], device_id=at(g, far), device_id_type=MESH)
        for k in range(pieces)
    ]
    weight_copy = pltpu.make_async_remote_copy(
        src_ref=potential.at[pl.ds(pl.multiple_of(far * rows, rows), rows), :], dst_ref=guest_weights,
        send_sem=guest_send.at[pieces + 1], recv_sem=guest_recv.at[pieces + 1],
        device_id=at(g, host), device_id_type=MESH)

    @pl.when(edge)
    def _():
        far_group = every_group[jnp.where(z == 0, 1, last)]
        for k in range(pieces):
            columns = pl.ds(k * cut, cut)
            far_leaving[:, columns] = pick(far_group, own_start, slab[z, :, columns]).astype(jnp.bfloat16)
            far_copies[k].start()
        for k in range(early, pieces):
            send_line(k, 0)
        weight_copy.start()

    place = pl.ds(pl.multiple_of(g * count, count), count)
    grid_copies = []

    def spread_copies(ref, sends, recvs):
        return [
            pltpu.make_async_remote_copy(
                src_ref=ref, dst_ref=ref, send_sem=sends.at[step - 1], recv_sem=recvs.at[step - 1],
                device_id=at(other(g, step, slabs), z), device_id_type=MESH)
            for step in range(1, slabs)
        ]

    def spread(ref, sends, recvs):
        copies = spread_copies(ref, sends, recvs)
        for copy in copies:
            copy.start()
        grid_copies.extend(copies)

    guest_copies = [
        pltpu.make_async_remote_copy(
            src_ref=orbital_values.at[place, pl.ds(k * cut, cut)],
            dst_ref=guest_orbitals.at[place, pl.ds(k * cut, cut)],
            send_sem=guest_send.at[k], recv_sem=guest_recv.at[k], device_id=at(g, host), device_id_type=MESH)
        for k in range(pieces)
    ]
    guest_copies.append(pltpu.make_async_remote_copy(
        src_ref=target_values.at[place, :], dst_ref=guest_targets.at[place, :],
        send_sem=guest_send.at[pieces], recv_sem=guest_recv.at[pieces],
        device_id=at(g, host), device_id_type=MESH))
    pass_copies = [
        spread_copies(guest_orbitals.at[place, pl.ds(k * cut, cut)], pass_send.at[k], pass_recv.at[k])
        for k in range(pieces)
    ]
    pass_copies.append(spread_copies(guest_targets.at[place, :], pass_send.at[pieces], pass_recv.at[pieces]))

    def pass_on(k):
        @pl.when(hosting)
        def _():
            guest_copies[k].wait_recv()
            for copy in pass_copies[k]:
                copy.start()

    for s in range(pieces + groups - 2):
        for d in range(groups - 1):
            k = s - d
            if not 0 <= k < pieces:
                continue
            if d > 0:
                await_line(k, d)
            if d == 0 and k > 0:
                pl.when(jnp.logical_not(edge))(functools.partial(send_line, k, 0))
            elif 0 < d < groups - 2:
                send_line(k, d)
        k = s - (groups - 2)
        if k < 0:
            continue
        columns = pl.ds(k * cut, cut)
        def pick_chunk(chunk):
            return pick(every_group[0], slab_start + chunk * rows, slab[chunk, :, columns])

        piece_sum[...] = sum(pick_chunk(chunk) for chunk in range(1, last))

        @pl.when(z != last)
        def _():
            piece_sum[...] += pick_chunk(0)

        @pl.when(z != 0)
        def _():
            piece_sum[...] += pick_chunk(last)

        @pl.when(edge)
        def _():
            far_copies[k].wait_recv()
            piece_sum[...] += far_values[:, columns].astype(jnp.float32)

        orbital_values[place, columns] = piece_sum[...].astype(jnp.bfloat16)
        pl.when(edge)(guest_copies[k].start)
        spread(orbital_values.at[place, columns], grid_send.at[k], grid_recv.at[k])
        if k == 0:
            values = own_pick
            for step in range(1, groups):
                pick_copies[step - 1].wait()
                values += landed[step - 1].astype(jnp.float32)
            target_values[place, :] = values.astype(jnp.bfloat16)
            pl.when(edge)(guest_copies[pieces].start)
            spread(target_values.at[place, :], value_send, value_recv)
            pass_on(pieces)
        else:
            pass_on(k - 1)
    pass_on(pieces - 1)

    own_weights.wait()
    for copy in grid_copies:
        copy.wait_recv()

    def add(chunk, values, target_piece, kernel_ref, first_row):
        @pl.loop(0, slabs * count // WIDTH)
        def _(b):
            block = pl.ds(pl.multiple_of(b * WIDTH, WIDTH), WIDTH)
            products = lax.dot_general(
                slab[chunk], values[block, :], (((1,), (1,)), ((), ())), preferred_element_type=jnp.float32)
            kernel_rows = kernel_ref[pl.ds(pl.multiple_of(first_row, rows), rows), block]
            weighted = (kernel_rows.astype(jnp.float32) * products).astype(jnp.bfloat16)
            total[...] += jnp.dot(weighted, target_piece[block, :], preferred_element_type=jnp.float32)

    def add_own(chunk):
        total[...] = jnp.zeros_like(total)
        add(chunk, orbital_values, target_values, weights, chunk * rows)

    def sum_copy(n, chunk):
        return pltpu.make_async_remote_copy(
            src_ref=leaving.at[n], dst_ref=arriving.at[n], send_sem=sum_send.at[n], recv_sem=sum_recv.at[n],
            device_id=at(g, chunk), device_id_type=MESH)

    def left_out(one, two):
        return ((one == 0) & (two == last)) | ((one == last) & (two == 0))

    middle = groups // 2
    for step in [n for n in range(1, groups) if n != middle] + [middle]:
        chunk = other(z, step, groups)

        @pl.when(jnp.logical_not(left_out(z, chunk)))
        def _():
            add_own(chunk)

            @pl.when(hosting & (chunk == guest_chunk))
            def _():
                for copies in pass_copies:
                    for copy in copies:
                        copy.wait_recv()
                weight_copy.wait_recv()
                add(guest_chunk, guest_orbitals, guest_targets, guest_weights, 0)

            leaving[step - 1] = total[...].astype(jnp.bfloat16)
            sum_copy(step - 1, chunk).start()

    add_own(z)
    for step in range(1, groups):
        @pl.when(jnp.logical_not(left_out(z, other(z, groups - step, groups))))
        def _():
            sum_copy(step - 1, z).wait_recv()
            total[...] += arriving[step - 1].astype(jnp.float32)
    out[...] = (-total[...]).astype(out.dtype)

    for step in range(1, groups):
        chunk = other(z, step, groups)
        pl.when(jnp.logical_not(left_out(z, chunk)))(sum_copy(step - 1, chunk).wait_send)

    @pl.when(edge)
    def _():
        for copy in far_copies + guest_copies + [weight_copy]:
            copy.wait_send()

    @pl.when(hosting)
    def _():
        for copies in pass_copies:
            for copy in copies:
                copy.wait_send()

    for k in range(pieces):
        for d in range(groups - 2):
            for valid, copy in (up(k, d), down(k, d)):
                pl.when(valid)(copy.wait_send)
    for copy in grid_copies:
        copy.wait_send()


def local(orbitals, targets, points, potential):
    groups, slabs = lax.axis_size("ipts"), lax.axis_size("grid")
    rows, norb = orbitals.shape
    nj = targets.shape[1]
    count = points.shape[1]
    pieces = max(norb // 256, 1)
    dma, bf16 = pltpu.SemaphoreType.DMA, jnp.bfloat16
    return pl.pallas_call(
        functools.partial(kernel, groups, slabs, pieces),
        out_shape=jax.ShapeDtypeStruct((rows, nj), bf16),
        in_specs=[pl.BlockSpec(memory_space=pl.ANY)] * 4,
        out_specs=pl.BlockSpec(memory_space=pltpu.VMEM),
        scratch_shapes=[
            pltpu.VMEM((groups, rows, norb), bf16),
            pltpu.VMEM((slabs * count, norb), bf16),
            pltpu.VMEM((slabs * count, nj), bf16),
            pltpu.VMEM(potential.shape, bf16),
            pltpu.VMEM((rows, nj), bf16),
            pltpu.VMEM((groups, 1, count), jnp.int32),
            pltpu.VMEM((groups - 1, count, nj), bf16),
            pltpu.VMEM((groups - 1, count, nj), bf16),
            pltpu.VMEM((rows, nj), jnp.float32),
            pltpu.VMEM((groups - 1, rows, nj), bf16),
            pltpu.VMEM((groups - 1, rows, nj), bf16),
            pltpu.VMEM((count, norb // pieces), jnp.float32),
            pltpu.VMEM((count, norb), bf16),
            pltpu.VMEM((count, norb), bf16),
            pltpu.VMEM((slabs * count, norb), bf16),
            pltpu.VMEM((slabs * count, nj), bf16),
            pltpu.VMEM((rows, potential.shape[1]), bf16),
            dma((pieces + 3,)),
            dma((pieces, groups - 1)),
            dma((pieces, groups - 1)),
            dma((pieces, groups)),
            dma((pieces, slabs - 1)),
            dma((pieces, slabs - 1)),
            dma((groups - 1,)),
            dma((groups - 1,)),
            dma((groups - 1,)),
            dma((groups - 1,)),
            dma((slabs - 1,)),
            dma((slabs - 1,)),
            dma((groups - 1,)),
            dma((groups - 1,)),
            dma((pieces,)),
            dma((pieces,)),
            dma((pieces + 2,)),
            dma((pieces + 2,)),
            dma((pieces + 1, slabs - 1)),
            dma((pieces + 1, slabs - 1)),
        ],
        compiler_params=pltpu.CompilerParams(
            collective_id=0, has_side_effects=True, vmem_limit_bytes=60 * 1024 * 1024),
    )(orbitals, targets, points, potential)


def solution(mesh):
    placed = (
        P(("grid", "ipts"), None),
        P(("grid", "ipts"), None),
        P("ipts", "grid"),
        P("grid", "ipts"),
    )
    return jax.shard_map(
        local, mesh=mesh, in_specs=placed, out_specs=P(("grid", "ipts"), None), check_vma=False
    )
```

```python
import functools

import jax
import jax.numpy as jnp
from jax import lax
from jax.experimental import pallas as pl
from jax.experimental.pallas import tpu as pltpu
from jax.sharding import PartitionSpec as P

MESH = pl.DeviceIdType.MESH
WIDTH = 256


def kernel(groups, slabs, pieces, orbitals, targets, points, potential, out,
           slab, orbital_values, target_values, weights, target_rows, every_group, picked, landed,
           total, leaving, arriving, piece_sum, far_leaving, far_values,
           guest_orbitals, guest_targets, guest_weights,
           local_sem, up_sem, down_sem, row_sem, grid_send, grid_recv, index_send, index_recv,
           pick_send, pick_recv, value_send, value_recv, sum_send, sum_recv,
           far_send, far_recv, guest_send, guest_recv, pass_send, pass_recv):
    g = lax.axis_index("grid")
    z = lax.axis_index("ipts")
    rows, norb = orbitals.shape
    nj = targets.shape[1]
    count = points.shape[1]
    cut = norb // pieces
    last = groups - 1
    edge = (z == 0) | (z == last)
    hosting = (z == 1) | (z == last - 1)
    host = jnp.where(z == 0, 1, last - 1)
    far = jnp.where(z == 0, last, 0)
    guest_chunk = jnp.where(z == 1, last, 0)

    def at(grid, group):
        return {"grid": grid, "ipts": group}

    def other(base, step, size):
        return lax.rem(base + step, size)

    own = [
        pltpu.make_async_copy(
            orbitals.at[:, pl.ds(k * cut, cut)], slab.at[z, :, pl.ds(k * cut, cut)], local_sem.at[k])
        for k in range(pieces)
    ]
    own_targets = pltpu.make_async_copy(targets, target_rows, local_sem.at[pieces])
    own_points = pltpu.make_async_copy(points, every_group.at[0], local_sem.at[pieces + 1])
    own_weights = pltpu.make_async_copy(potential, weights, local_sem.at[pieces + 2])
    own_points.start()
    for copy in own:
        copy.start()
    own_targets.start()
    own_weights.start()

    barrier = pltpu.get_barrier_semaphore()
    for step in range(1, groups):
        pl.semaphore_signal(barrier, inc=1, device_id=at(g, other(z, step, groups)), device_id_type=MESH)
    for step in range(1, slabs):
        pl.semaphore_signal(barrier, inc=1, device_id=at(other(g, step, slabs), z), device_id_type=MESH)
    pl.semaphore_wait(barrier, groups + slabs - 2)

    def line_copy(k, chunk, sem, target):
        block = slab.at[chunk, :, pl.ds(k * cut, cut)]
        return pltpu.make_async_remote_copy(
            src_ref=block, dst_ref=block, send_sem=sem, recv_sem=row_sem.at[k, chunk],
            device_id=at(g, target), device_id_type=MESH)

    def up(k, d):
        return (z - d >= 0) & (z + 1 < groups), line_copy(
            k, jnp.maximum(z - d, 0), up_sem.at[k, d], jnp.minimum(z + 1, groups - 1))

    def down(k, d):
        return (z + d < groups) & (z >= 1), line_copy(
            k, jnp.minimum(z + d, groups - 1), down_sem.at[k, d], jnp.maximum(z - 1, 0))

    def send_line(k, d):
        for valid, copy in (up(k, d), down(k, d)):
            pl.when(valid)(copy.start)

    def await_line(k, d):
        pl.when(z - d >= 0)(lambda: line_copy(k, jnp.maximum(z - d, 0), up_sem.at[k, 0], z).wait_recv())
        pl.when(z + d < groups)(
            lambda: line_copy(k, jnp.minimum(z + d, groups - 1), up_sem.at[k, 0], z).wait_recv())

    early = min(2, pieces)
    for copy in own:
        copy.wait()
    send_line(0, 0)

    @pl.when(edge)
    def _():
        for k in range(1, early):
            send_line(k, 0)

    own_points.wait()
    index_copies = [
        pltpu.make_async_remote_copy(
            src_ref=every_group.at[0], dst_ref=every_group.at[step],
            send_sem=index_send.at[step - 1], recv_sem=index_recv.at[step - 1],
            device_id=at(g, other(z, step, groups)), device_id_type=MESH)
        for step in range(1, groups)
    ]
    for copy in index_copies:
        copy.start()

    slab_start = g * rows * groups

    def chosen(indices, start, length):
        place = lax.broadcasted_iota(jnp.int32, (length, count), 0) + start
        return (place == indices).astype(jnp.float32).astype(jnp.bfloat16)

    def pick(indices, start, block):
        return lax.dot_general(
            chosen(indices, start, block.shape[0]), block, (((0,), (0,)), ((), ())),
            preferred_element_type=jnp.float32)

    own_targets.wait()
    own_start = slab_start + z * rows
    pick_copies = []
    own_pick = pick(every_group[0], own_start, target_rows[...])
    for step in range(1, groups):
        index_copies[step - 1].wait()
        picked[step - 1] = pick(every_group[step], own_start, target_rows[...]).astype(jnp.bfloat16)
        copy = pltpu.make_async_remote_copy(
            src_ref=picked.at[step - 1], dst_ref=landed.at[step - 1],
            send_sem=pick_send.at[step - 1], recv_sem=pick_recv.at[step - 1],
            device_id=at(g, other(z, groups - step, groups)), device_id_type=MESH)
        copy.start()
        pick_copies.append(copy)

    far_copies = [
        pltpu.make_async_remote_copy(
            src_ref=far_leaving.at[:, pl.ds(k * cut, cut)], dst_ref=far_values.at[:, pl.ds(k * cut, cut)],
            send_sem=far_send.at[k], recv_sem=far_recv.at[k], device_id=at(g, far), device_id_type=MESH)
        for k in range(pieces)
    ]
    share = rows // pieces
    weight_copies = [
        pltpu.make_async_remote_copy(
            src_ref=potential.at[pl.ds(pl.multiple_of(far * rows + k * share, share), share), :],
            dst_ref=guest_weights.at[pl.ds(k * share, share), :],
            send_sem=guest_send.at[pieces + 1 + k], recv_sem=guest_recv.at[pieces + 1 + k],
            device_id=at(g, host), device_id_type=MESH)
        for k in range(pieces)
    ]

    @pl.when(edge)
    def _():
        far_group = every_group[jnp.where(z == 0, 1, last)]
        for k in range(pieces):
            columns = pl.ds(k * cut, cut)
            far_leaving[:, columns] = pick(far_group, own_start, slab[z, :, columns]).astype(jnp.bfloat16)
            far_copies[k].start()
        for k in range(early, pieces):
            send_line(k, 0)

    place = pl.ds(pl.multiple_of(g * count, count), count)
    grid_copies = []

    def spread_copies(ref, sends, recvs):
        return [
            pltpu.make_async_remote_copy(
                src_ref=ref, dst_ref=ref, send_sem=sends.at[step - 1], recv_sem=recvs.at[step - 1],
                device_id=at(other(g, step, slabs), z), device_id_type=MESH)
            for step in range(1, slabs)
        ]

    def spread(ref, sends, recvs):
        copies = spread_copies(ref, sends, recvs)
        for copy in copies:
            copy.start()
        grid_copies.extend(copies)

    guest_copies = [
        pltpu.make_async_remote_copy(
            src_ref=orbital_values.at[place, pl.ds(k * cut, cut)],
            dst_ref=guest_orbitals.at[place, pl.ds(k * cut, cut)],
            send_sem=guest_send.at[k], recv_sem=guest_recv.at[k], device_id=at(g, host), device_id_type=MESH)
        for k in range(pieces)
    ]
    guest_copies.append(pltpu.make_async_remote_copy(
        src_ref=target_values.at[place, :], dst_ref=guest_targets.at[place, :],
        send_sem=guest_send.at[pieces], recv_sem=guest_recv.at[pieces],
        device_id=at(g, host), device_id_type=MESH))
    pass_copies = [
        spread_copies(guest_orbitals.at[place, pl.ds(k * cut, cut)], pass_send.at[k], pass_recv.at[k])
        for k in range(pieces)
    ]
    pass_copies.append(spread_copies(guest_targets.at[place, :], pass_send.at[pieces], pass_recv.at[pieces]))

    def pass_on(k):
        @pl.when(hosting)
        def _():
            guest_copies[k].wait_recv()
            for copy in pass_copies[k]:
                copy.start()

    for s in range(pieces + groups - 2):
        for d in range(groups - 1):
            k = s - d
            if not 0 <= k < pieces:
                continue
            if d > 0:
                await_line(k, d)
            if d == 0 and k > 0:
                pl.when(jnp.logical_not(edge))(functools.partial(send_line, k, 0))
            elif 0 < d < groups - 2:
                send_line(k, d)
        k = s - (groups - 2)
        if k < 0:
            continue
        columns = pl.ds(k * cut, cut)
        def pick_chunk(chunk):
            return pick(every_group[0], slab_start + chunk * rows, slab[chunk, :, columns])

        piece_sum[...] = sum(pick_chunk(chunk) for chunk in range(1, last))

        @pl.when(z != last)
        def _():
            piece_sum[...] += pick_chunk(0)

        @pl.when(z != 0)
        def _():
            piece_sum[...] += pick_chunk(last)

        @pl.when(edge)
        def _():
            far_copies[k].wait_recv()
            piece_sum[...] += far_values[:, columns].astype(jnp.float32)

        orbital_values[place, columns] = piece_sum[...].astype(jnp.bfloat16)

        @pl.when(edge)
        def _():
            guest_copies[k].start()
            for part in range(pieces):
                if k == min(part, max(pieces - 2, 0)):
                    weight_copies[part].start()

        spread(orbital_values.at[place, columns], grid_send.at[k], grid_recv.at[k])
        if k == 0:
            values = own_pick
            for step in range(1, groups):
                pick_copies[step - 1].wait()
                values += landed[step - 1].astype(jnp.float32)
            target_values[place, :] = values.astype(jnp.bfloat16)
            pl.when(edge)(guest_copies[pieces].start)
            spread(target_values.at[place, :], value_send, value_recv)
            pass_on(pieces)
        else:
            pass_on(k - 1)
    pass_on(pieces - 1)

    own_weights.wait()
    for copy in grid_copies:
        copy.wait_recv()

    def add(chunk, values, target_piece, kernel_ref, first_row):
        @pl.loop(0, slabs * count // WIDTH)
        def _(b):
            block = pl.ds(pl.multiple_of(b * WIDTH, WIDTH), WIDTH)
            products = lax.dot_general(
                slab[chunk], values[block, :], (((1,), (1,)), ((), ())), preferred_element_type=jnp.float32)
            kernel_rows = kernel_ref[pl.ds(pl.multiple_of(first_row, rows), rows), block]
            weighted = (kernel_rows.astype(jnp.float32) * products).astype(jnp.bfloat16)
            total[...] += jnp.dot(weighted, target_piece[block, :], preferred_element_type=jnp.float32)

    def add_own(chunk):
        total[...] = jnp.zeros_like(total)
        add(chunk, orbital_values, target_values, weights, chunk * rows)

    def sum_copy(n, chunk):
        return pltpu.make_async_remote_copy(
            src_ref=leaving.at[n], dst_ref=arriving.at[n], send_sem=sum_send.at[n], recv_sem=sum_recv.at[n],
            device_id=at(g, chunk), device_id_type=MESH)

    def left_out(one, two):
        return ((one == 0) & (two == last)) | ((one == last) & (two == 0))

    middle = groups // 2
    for step in [n for n in range(1, groups) if n != middle] + [middle]:
        chunk = other(z, step, groups)

        @pl.when(jnp.logical_not(left_out(z, chunk)))
        def _():
            add_own(chunk)

            @pl.when(hosting & (chunk == guest_chunk))
            def _():
                for copies in pass_copies:
                    for copy in copies:
                        copy.wait_recv()
                for copy in weight_copies:
                    copy.wait_recv()
                add(guest_chunk, guest_orbitals, guest_targets, guest_weights, 0)

            leaving[step - 1] = total[...].astype(jnp.bfloat16)
            sum_copy(step - 1, chunk).start()

    add_own(z)
    for step in range(1, groups):
        @pl.when(jnp.logical_not(left_out(z, other(z, groups - step, groups))))
        def _():
            sum_copy(step - 1, z).wait_recv()
            total[...] += arriving[step - 1].astype(jnp.float32)
    out[...] = (-total[...]).astype(out.dtype)

    for step in range(1, groups):
        chunk = other(z, step, groups)
        pl.when(jnp.logical_not(left_out(z, chunk)))(sum_copy(step - 1, chunk).wait_send)

    @pl.when(edge)
    def _():
        for copy in far_copies + guest_copies + weight_copies:
            copy.wait_send()

    @pl.when(hosting)
    def _():
        for copies in pass_copies:
            for copy in copies:
                copy.wait_send()

    for k in range(pieces):
        for d in range(groups - 2):
            for valid, copy in (up(k, d), down(k, d)):
                pl.when(valid)(copy.wait_send)
    for copy in grid_copies:
        copy.wait_send()


def local(orbitals, targets, points, potential):
    groups, slabs = lax.axis_size("ipts"), lax.axis_size("grid")
    rows, norb = orbitals.shape
    nj = targets.shape[1]
    count = points.shape[1]
    pieces = max(norb // 256, 1)
    dma, bf16 = pltpu.SemaphoreType.DMA, jnp.bfloat16
    return pl.pallas_call(
        functools.partial(kernel, groups, slabs, pieces),
        out_shape=jax.ShapeDtypeStruct((rows, nj), bf16),
        in_specs=[pl.BlockSpec(memory_space=pl.ANY)] * 4,
        out_specs=pl.BlockSpec(memory_space=pltpu.VMEM),
        scratch_shapes=[
            pltpu.VMEM((groups, rows, norb), bf16),
            pltpu.VMEM((slabs * count, norb), bf16),
            pltpu.VMEM((slabs * count, nj), bf16),
            pltpu.VMEM(potential.shape, bf16),
            pltpu.VMEM((rows, nj), bf16),
            pltpu.VMEM((groups, 1, count), jnp.int32),
            pltpu.VMEM((groups - 1, count, nj), bf16),
            pltpu.VMEM((groups - 1, count, nj), bf16),
            pltpu.VMEM((rows, nj), jnp.float32),
            pltpu.VMEM((groups - 1, rows, nj), bf16),
            pltpu.VMEM((groups - 1, rows, nj), bf16),
            pltpu.VMEM((count, norb // pieces), jnp.float32),
            pltpu.VMEM((count, norb), bf16),
            pltpu.VMEM((count, norb), bf16),
            pltpu.VMEM((slabs * count, norb), bf16),
            pltpu.VMEM((slabs * count, nj), bf16),
            pltpu.VMEM((rows, potential.shape[1]), bf16),
            dma((pieces + 3,)),
            dma((pieces, groups - 1)),
            dma((pieces, groups - 1)),
            dma((pieces, groups)),
            dma((pieces, slabs - 1)),
            dma((pieces, slabs - 1)),
            dma((groups - 1,)),
            dma((groups - 1,)),
            dma((groups - 1,)),
            dma((groups - 1,)),
            dma((slabs - 1,)),
            dma((slabs - 1,)),
            dma((groups - 1,)),
            dma((groups - 1,)),
            dma((pieces,)),
            dma((pieces,)),
            dma((2 * pieces + 1,)),
            dma((2 * pieces + 1,)),
            dma((pieces + 1, slabs - 1)),
            dma((pieces + 1, slabs - 1)),
        ],
        compiler_params=pltpu.CompilerParams(
            collective_id=0, has_side_effects=True, vmem_limit_bytes=60 * 1024 * 1024),
    )(orbitals, targets, points, potential)


def solution(mesh):
    placed = (
        P(("grid", "ipts"), None),
        P(("grid", "ipts"), None),
        P("ipts", "grid"),
        P("grid", "ipts"),
    )
    return jax.shard_map(
        local, mesh=mesh, in_specs=placed, out_specs=P(("grid", "ipts"), None), check_vma=False
    )
```
